32 devices in a mesh: group: 1, wide: 32 (over z, y, x, core).
Axes of the slice: x: 2, y: 2, z: 4, core: 2. Of those that a mesh axis runs over, the one named last changes fastest.
Arguments:
- ssd_x: bfloat16 [2048, 4096], P(('group', 'wide')), may hold values from -6 to 6
- ssd_z: bfloat16 [2048, 4096], P(('group', 'wide')), may hold values from -6 to 6
- ssd_b: bfloat16 [2048, 128], P(('group', 'wide')), may hold values from -2 to 2
- ssd_c: bfloat16 [2048, 128], P(('group', 'wide')), may hold values from -2 to 2
- dt_raw: bfloat16 [2048, 64], P(('group', 'wide')), may hold values from -4 to 4
- dt_bias: float32 [64], replicated, may hold values from -4 to -1
- a_log: float32 [64], replicated, may hold values from -1.5 to 1.5
- d_skip: float32 [64], replicated, may hold values from 0.5 to 1.5
- norm_gain: float32 [4096], replicated, may hold values from 0.1 to 1.9
- cache_state: bfloat16 [64, 64, 64, 128], P(('group', 'wide')), may hold values from -2 to 2
- cache_owner: int32 [64], P('group'), may hold values from 0 to 63
- resid: bfloat16 [2048, 2048], P(('group', 'wide')), may hold values from -3 to 3
- w_out: bfloat16 [4096, 2048], P('wide'), may hold values from -0.09375 to 0.09375
- moe_gain: float32 [2048], replicated, may hold values from 0.1 to 1.9
- expert_ids: int32 [2048, 10], P(('group', 'wide')), may hold values from 0 to 31, all different within a row; in each aligned block of 64 rows (0 to 63, 64 to 127, ...) at most 32 rows name the same one
- route_weight: int32 [2048, 10], P(('group', 'wide')), may hold values from 1 to 1023
- expert_home: int32 [32], replicated, may hold values from 0 to 31, each once
- w_gate: bfloat16 [32, 2048, 384], P('wide'), may hold values from -0.125 to 0.125
- w_up: bfloat16 [32, 2048, 384], P('wide'), may hold values from -0.125 to 0.125
- w_down: bfloat16 [32, 384, 2048], P('wide'), may hold values from -0.3125 to 0.3125
Outputs:
- ssd_out: bfloat16 [2048, 4096], P(('group', 'wide'))
- moe_out: bfloat16 [2048, 2048], P(('group', 'wide'))
The draws below stay inside these ranges and needn't reach their ends.
Inputs may be any that keep to these rules, and one draw needn't show every extreme that they name: `cache_owner`: slot s of cache_state holds a cached prefix state; several requests may continue from the same slot. `expert_ids`: each token names 10 different experts. In each aligned block of 64 tokens (the tokens of one device) no expert is named by more than 32 tokens, and in every draw some expert is named by exactly 32 tokens of some block. `expert_home`: A permutation of the experts.
All inputs are finite; a program needn't handle non-finite values.
Results may differ from the reference program's by a relative error of at most 0.02.
Values may be sent and summed in bfloat16 or wider, within the bound.
No kernel may reach another device: no remote copies, remote signals or barrier semaphores. Data moves between devices by JAX's collectives and lax.ppermute only.
A program may use at most 128 MiB of HBM per device.

```python
import math
import jax
import jax.numpy as jnp
import numpy as np
from jax import lax

D = 2048
HEADS = 64
HEAD_DIM = 64
STATE = 128
EXP_HID = 384
TOPK = 10
SEQ = 32
TOK_DEV = 64
REQUESTS = 64
SLOTS = 64
TOKENS = 2048
EXPERTS = 32
CAP = 32
N_WIDE = 32


def with_ends(array, rng, smallest, largest):
    spot = [jax.random.randint(jax.random.fold_in(rng, axis), (), 0, length) for axis, length in enumerate(array.shape)]
    longest = array.shape.index(max(array.shape))
    neighbour = spot[:longest] + [(spot[longest] + 1) % array.shape[longest]] + spot[longest + 1:]
    return array.at[tuple(spot)].set(smallest).at[tuple(neighbour)].set(largest)


def steps_of(key, extent, pieces, least, top_value):
    def one(axis_at, shards_of):
        heights = jax.random.uniform(jax.random.fold_in(jax.random.fold_in(key, 6), axis_at), (shards_of,), jnp.float32, least / len(pieces), top_value / len(pieces))
        return jnp.repeat(jnp.exp(heights), extent[axis_at] // shards_of).reshape((-1,) + (1,) * (len(extent) - axis_at - 1))

    loudness = one(*pieces[0])
    for cut in pieces[1:]:
        loudness = loudness * one(*cut)
    return loudness


def shared_out(rng, own, number, rows, number_of, top, bound, slope):
    order = jax.random.permutation(rng, number_of)
    crowded, ordinary = portions_of(number_of, rows * top, bound, slope, True), portions_of(number_of, rows * top, bound, slope, False)
    places = jnp.arange(number_of)

    def named(lengths, offset_by):
        used = int((lengths > 0).sum())
        fixed = max(1, used // 4)
        moved = fixed + (places - fixed + offset_by * (used - fixed)) % max(1, number_of - fixed)
        return jnp.zeros((number_of,), jnp.int32).at[order[jnp.where(places < fixed, places, moved)]].set(jnp.asarray(lengths, jnp.int32))

    lengths = jnp.where(number % 4 == 0, named(crowded, number // 4), named(ordinary, number - number // 4 - 1))
    mixed = jax.random.permutation(jax.random.fold_in(own, 3), number_of)
    giver, taker = mixed[0:number_of // 2 * 2:2], mixed[1:number_of // 2 * 2:2]
    margin = jnp.minimum(lengths[giver] - 1, bound - lengths[taker]) // 2
    margin = jnp.where((giver == order[0]) | (taker == order[0]) | (lengths[taker] == 0), 0, jnp.maximum(margin, 0))
    moved = jax.random.randint(jax.random.fold_in(own, 4), (number_of // 2,), 0, 1 << 20) % (margin + 1)
    lengths = lengths.at[giver].add(-moved).at[taker].add(moved)
    members = jnp.searchsorted(jnp.cumsum(lengths), jnp.arange(rows * top), side="right").astype(jnp.int32)
    table = members.reshape(top, rows).T
    table = table[jax.random.permutation(jax.random.fold_in(own, 1), rows)]
    offset_by = jax.random.randint(jax.random.fold_in(own, 2), (rows, 1), 0, top)
    return jnp.take_along_axis(table, (jnp.arange(top)[None, :] + offset_by) % top, axis=1)


def portions_of(count, total, most, slope, full):
    loads = [(1 << 20) // math.isqrt(standing ** slope) + 1 for standing in range(1, count + 1)]
    largest = most if full else min(most, max(-(-total // count), total * loads[0] // sum(loads)))
    least = 1 if total - largest >= count - 1 else 0
    holding, rest = [largest] + [least] * (count - 1), total - largest - least * (count - 1)
    while rest > 0:
        movable = [i for i in range(1, count) if holding[i] < largest] or [i for i in range(1, count) if holding[i] < most]
        mass, left = sum([loads[i] for i in movable]), rest
        for i in movable:
            more = min(most - holding[i], max(1, left * loads[i] // mass), rest)
            holding[i] = holding[i] + more
            rest = rest - more
    return np.array(holding)


def noise(stream_key, shape, deviation, most, cuts=(), held_as=jnp.bfloat16):
    loudness = steps_of(stream_key, shape, cuts, -0.22, 0.18) if cuts else 1.0
    values = jax.random.normal(stream_key, shape, jnp.float32) * deviation * loudness
    return jnp.minimum(jnp.maximum(values, -most), most).astype(held_as)


def setup_inputs(seed: int = 0, part: int = 0) -> dict:
    seeds = jax.random.split(jax.random.key(seed), 21)
    part_keys = jax.random.split(jax.random.fold_in(seeds[20], part), 21)
    ssd_x = noise(part_keys[0], (TOKENS, HEADS * HEAD_DIM), 1.0, 6.0, ((0, 32),))
    ssd_z = noise(part_keys[1], (TOKENS, HEADS * HEAD_DIM), 1.0, 6.0, ((0, 32),))
    ssd_b = noise(part_keys[2], (TOKENS, STATE), 0.35, 2.0, ((0, 32),))
    ssd_c = noise(part_keys[3], (TOKENS, STATE), 0.35, 2.0, ((0, 32),))
    dt_raw = noise(part_keys[4], (TOKENS, HEADS), 1.0, 4.0, ((0, 32),))
    dt_bias = jnp.clip(jax.random.uniform(seeds[5], (HEADS,), jnp.float32, -4.0, -1.0), -4.0, -1.0)
    a_log = jnp.clip(jax.random.uniform(seeds[6], (HEADS,), jnp.float32, -1.5, 1.5), -1.5, 1.5)
    d_skip = jnp.clip(jax.random.uniform(seeds[7], (HEADS,), jnp.float32, 0.5, 1.5), 0.5, 1.5)
    norm_gain = jnp.clip(1.0 + 0.18 * jax.random.normal(seeds[8], (HEADS * HEAD_DIM,), jnp.float32), 0.1, 1.9)
    cache_state = noise(part_keys[9], (SLOTS, HEADS, HEAD_DIM, STATE), 0.3, 2.0, ((0, 32),))
    cache_owner = with_ends(jax.random.randint(part_keys[10], (REQUESTS,), 0, SLOTS), jax.random.fold_in(part_keys[10], 1), 0, SLOTS - 1).astype(jnp.int32)
    resid = noise(part_keys[11], (TOKENS, D), 0.5, 3.0, ((0, 32),))
    w_out = noise(seeds[12], (HEADS * HEAD_DIM, D), (HEADS * HEAD_DIM) ** -0.5, 0.09375, ((0, 32),))
    moe_gain = jnp.clip(1.0 + 0.18 * jax.random.normal(seeds[13], (D,), jnp.float32), 0.1, 1.9)
    expert_ids_keys = jax.random.split(jax.random.fold_in(part_keys[14], 1), TOKENS // TOK_DEV)
    expert_ids_turns = jax.random.permutation(jax.random.fold_in(part_keys[14], 3), TOKENS // TOK_DEV)
    expert_ids = jax.vmap(lambda own, number: shared_out(jax.random.fold_in(part_keys[14], 2), own, number, TOK_DEV, EXPERTS, TOPK, CAP, 2))(expert_ids_keys, expert_ids_turns).reshape((TOKENS, TOPK))
    route_weight = with_ends(jax.random.randint(part_keys[15], (TOKENS, TOPK), 1, 1024), jax.random.fold_in(part_keys[15], 1), 1, 1023).astype(jnp.int32)
    expert_home = jax.random.permutation(seeds[16], EXPERTS).astype(jnp.int32)
    w_gate = noise(seeds[17], (EXPERTS, D, EXP_HID), D ** -0.5, 0.125, ((0, 32),))
    w_up = noise(seeds[18], (EXPERTS, D, EXP_HID), D ** -0.5, 0.125, ((0, 32),))
    w_down = noise(seeds[19], (EXPERTS, EXP_HID, D), EXP_HID ** -0.5, 0.3125, ((0, 32),))
    return dict(ssd_x=ssd_x, ssd_z=ssd_z, ssd_b=ssd_b, ssd_c=ssd_c, dt_raw=dt_raw, dt_bias=dt_bias, a_log=a_log, d_skip=d_skip, norm_gain=norm_gain, cache_state=cache_state, cache_owner=cache_owner, resid=resid, w_out=w_out, moe_gain=moe_gain, expert_ids=expert_ids, route_weight=route_weight, expert_home=expert_home, w_gate=w_gate, w_up=w_up, w_down=w_down)


def intra_terms(inputs, step_size, cumulative, b_proj, c_proj, skip_gain):
    scores = jnp.einsum('rtn,rsn->rts', c_proj.astype(jnp.float32), b_proj.astype(jnp.float32))
    length = inputs.shape[1]
    causal = jnp.arange(length)[:, None] >= jnp.arange(length)[None, :]
    cum_heads = jnp.swapaxes(cumulative, 1, 2)
    log_gap = cum_heads[..., :, None] - cum_heads[..., None, :]
    decays = jnp.where(causal, jnp.exp(jnp.where(causal, log_gap, 0.0)), 0.0)
    mixing = scores[:, None] * decays * jnp.swapaxes(step_size, 1, 2)[:, :, None, :]
    mixing = lax.optimization_barrier(mixing.astype(jnp.bfloat16)).astype(jnp.float32)
    wide_in = inputs.astype(jnp.float32)
    result = jnp.einsum('rhts,rshp->rthp', mixing, wide_in) + skip_gain[None, None, :, None] * wide_in
    return result.astype(jnp.bfloat16)

def state_terms(c_proj, cumulative, start_state):
    product = jnp.einsum('rtn,rhpn->rthp', c_proj.astype(jnp.float32), start_state.astype(jnp.float32))
    return (product * jnp.exp(cumulative)[..., None]).astype(jnp.bfloat16)

def expert_mlp(row_set, gate_weight, up_weight, down_weight):
    gate_out = jnp.dot(row_set, gate_weight, preferred_element_type=jnp.float32)
    up_out = jnp.dot(row_set, up_weight, preferred_element_type=jnp.float32)
    hidden = (jax.nn.silu(gate_out) * up_out).astype(jnp.bfloat16)
    return jnp.dot(hidden, down_weight, preferred_element_type=jnp.float32).astype(jnp.bfloat16)

def reference(ssd_x, ssd_z, ssd_b, ssd_c, dt_raw, dt_bias, a_log, d_skip, norm_gain, cache_state, cache_owner, resid, w_out, moe_gain, expert_ids, route_weight, expert_home, w_gate, w_up, w_down):
    inputs = ssd_x.reshape(REQUESTS, SEQ, HEADS, HEAD_DIM)
    step_size = jax.nn.softplus(dt_raw.astype(jnp.float32) + dt_bias).reshape(REQUESTS, SEQ, HEADS)
    cumulative = jnp.cumsum(step_size * -jnp.exp(a_log), axis=1)
    b_proj = ssd_b.reshape(REQUESTS, SEQ, STATE)
    c_proj = ssd_c.reshape(REQUESTS, SEQ, STATE)
    intra = intra_terms(inputs, step_size, cumulative, b_proj, c_proj, d_skip)
    start_state = jnp.take(cache_state, cache_owner, axis=0)
    carried = state_terms(c_proj, cumulative, start_state)
    mixed = (intra.astype(jnp.float32) + carried.astype(jnp.float32)).reshape(TOKENS, HEADS * HEAD_DIM)
    gated = mixed * jax.nn.silu(ssd_z.astype(jnp.float32))
    ssd_out = (gated * lax.rsqrt(lax.optimization_barrier(jnp.mean(gated * gated, axis=-1, keepdims=True)) + 1e-05) * norm_gain).astype(jnp.bfloat16)
    wide_moe = resid.astype(jnp.float32) + jnp.dot(ssd_out, w_out, preferred_element_type=jnp.float32)
    normed = (wide_moe * lax.rsqrt(lax.optimization_barrier(jnp.mean(wide_moe * wide_moe, axis=-1, keepdims=True)) + 1e-05) * moe_gain).astype(jnp.bfloat16)
    weight_f = route_weight.astype(jnp.float32)
    share = weight_f / lax.optimization_barrier(jnp.sum(weight_f, axis=-1, keepdims=True))
    target = jnp.take(expert_home, expert_ids)
    limit = N_WIDE * CAP

    def one_expert(position, total):
        chosen = target == position
        weight_tok = lax.optimization_barrier(jnp.sum(jnp.where(chosen, share, 0.0), axis=-1))
        hit_any = jnp.any(chosen, axis=-1)
        picked = jnp.nonzero(hit_any, size=limit, fill_value=0)[0]
        valid = jnp.arange(limit) < jnp.sum(hit_any.astype(jnp.int32))
        outputs = expert_mlp(jnp.take(normed, picked, axis=0), w_gate[position], w_up[position], w_down[position])
        added = outputs.astype(jnp.float32) * jnp.where(valid, jnp.take(weight_tok, picked), 0.0)[:, None]
        return total.at[picked].add(added)
    total = lax.fori_loop(0, EXPERTS, one_expert, jnp.zeros((TOKENS, D), jnp.float32))
    return (ssd_out, total.astype(jnp.bfloat16))
```

```python
import functools

import jax
import jax.numpy as jnp
import numpy as np
from jax import lax
from jax.experimental import pallas as pl
from jax.experimental.pallas import tpu as pltpu
from jax.sharding import PartitionSpec as P

SEQ = 32

F32, BF16 = jnp.float32, jnp.bfloat16
Z, Y, X, CORE = 0, 1, 2, 3


def grid_of(mesh):
    wide = mesh.shape["wide"]
    line = np.asarray(mesh.devices).reshape(-1, wide)[0]
    try:
        places = [(d.coords[2], d.coords[1], d.coords[0], d.core_on_chip) for d in line]
    except (AttributeError, TypeError, IndexError):
        return (wide // 2, 1, 1, 2)
    ticks = [sorted({p[a] for p in places}) for a in range(4)]
    sizes = tuple(len(t) for t in ticks)
    ranks = [tuple(ticks[a].index(p[a]) for a in range(4)) for p in places]
    if int(np.prod(sizes)) == wide and sizes[CORE] == 2 and ranks == list(np.ndindex(*sizes)):
        return sizes
    return (wide // 2, 1, 1, 2)


class Moves:
    def __init__(self, sizes):
        self.sizes = sizes
        self.count = int(np.prod(sizes))

    def pairs(self, axis):
        out = []
        for i, place in enumerate(np.ndindex(*self.sizes)):
            to = list(place)
            to[axis] = (to[axis] + 1) % self.sizes[axis]
            out.append((i, int(np.ravel_multi_index(to, self.sizes))))
        return out

    def turn(self, value, axis):
        return lax.ppermute(value, "wide", self.pairs(axis))

    def ring(self, value, axis):
        held = [value]
        for _ in range(self.sizes[axis] - 1):
            held.append(self.turn(held[-1], axis))
        return held

    def fold(self, parts, axis):
        order = list(range(1, self.sizes[axis])) + [0]
        total = parts[order[0]]
        for k in order[1:]:
            total = self.turn(total.astype(BF16), axis).astype(F32) + parts[k].astype(F32)
        return total

    def gather(self, value, first, second):
        return [
            [self.ring(b, second) for b in self.ring(a, first)] for a in self.ring(value, Z)
        ]

    def plane_fold(self, blocks, first, second):
        return self.fold([self.fold(row, second) for row in blocks], first)


def intra_terms(inputs, step_size, cumulative, b_proj, c_proj, skip_gain):
    scores = jnp.einsum("rtn,rsn->rts", c_proj, b_proj, preferred_element_type=F32)
    length = inputs.shape[1]
    causal = jnp.arange(length)[:, None] >= jnp.arange(length)[None, :]
    cum_heads = jnp.swapaxes(cumulative, 1, 2)
    log_gap = cum_heads[..., :, None] - cum_heads[..., None, :]
    decays = jnp.where(causal, jnp.exp(jnp.where(causal, log_gap, 0.0)), 0.0)
    mixing = (scores[:, None] * decays * jnp.swapaxes(step_size, 1, 2)[:, :, None, :]).astype(BF16)
    result = jnp.einsum("rhts,rshp->rthp", mixing, inputs, preferred_element_type=F32)
    result = result + skip_gain[None, None, :, None] * inputs.astype(F32)
    return result.astype(BF16)


def head_steps(raw_steps, bias_part, rate_part, requests):
    step_size = jax.nn.softplus(raw_steps.astype(F32) + bias_part)
    step_size = step_size.reshape(requests, SEQ, step_size.shape[-1])
    return (step_size, jnp.cumsum(step_size * rate_part, axis=1))


def carried_kernel(owner, c_ref, state_ref, out_ref):
    def one(r, carry):
        state = state_ref[owner[r]]
        out_ref[r] = lax.dot_general(
            c_ref[r], state, (((1,), (1,)), ((), ())), preferred_element_type=F32
        ).astype(BF16)
        return carry

    lax.fori_loop(0, c_ref.shape[0], one, 0, unroll=8)


def carried_terms(owner, c_all, states):
    requests, length, _ = c_all.shape
    vmem = pl.BlockSpec(memory_space=pltpu.VMEM)
    return pl.pallas_call(
        carried_kernel,
        out_shape=jax.ShapeDtypeStruct((requests, length, states.shape[1]), BF16),
        in_specs=[pl.BlockSpec(memory_space=pltpu.SMEM), vmem, vmem],
        out_specs=vmem,
        name="carried",
    )(owner, c_all, states)


def project_kernel(cols, order, own_ref, sib_ref, *rest):
    count = len(cols)
    pieces, (own_out, sib_out, weight, rows, sems) = rest[:count], rest[count:]
    depth = own_ref.shape[2]
    blocks = order.shape[0]
    half = own_ref.shape[1]
    copies = []
    for i, (slot, col) in enumerate(cols):
        dst = weight.at[pl.ds(slot * depth, depth), pl.ds(col, pieces[i].shape[1])]
        copies.append(pltpu.make_async_copy(pieces[i], dst, sems.at[i]))
        copies[-1].start()
    for s in range(blocks):
        rows[pl.ds(0, half), pl.ds(s * depth, depth)] = own_ref[order[s]]
        rows[pl.ds(half, half), pl.ds(s * depth, depth)] = sib_ref[order[s]]
    group = 4 if blocks % 4 == 0 else 1
    total = None
    for g in range(blocks // group):
        for i, (slot, _) in enumerate(cols):
            if slot // group == g:
                copies[i].wait()
        at = pl.ds(g * group * depth, group * depth)
        part = jnp.dot(rows[:, at], weight[at, :], preferred_element_type=F32)
        total = part if total is None else total + part
    own_out[...] = total[:half]
    sib_out[...] = total[half:].astype(sib_out.dtype)


def project(order, own, sib, pieces):
    chips, tokens, depth = own.shape
    width = sum(p[2].shape[1] for p in pieces if p[0] == 0)
    vmem = pl.BlockSpec(memory_space=pltpu.VMEM)
    cols = tuple((p[0], p[1]) for p in pieces)
    return pl.pallas_call(
        functools.partial(project_kernel, cols),
        out_shape=(
            jax.ShapeDtypeStruct((tokens, width), F32),
            jax.ShapeDtypeStruct((tokens, width), F32),
        ),
        in_specs=[pl.BlockSpec(memory_space=pltpu.SMEM), vmem, vmem]
        + [pl.BlockSpec(memory_space=pl.ANY)] * len(pieces),
        out_specs=(vmem, vmem),
        scratch_shapes=[
            pltpu.VMEM((chips * depth, width), BF16),
            pltpu.VMEM((2 * tokens, chips * depth), BF16),
            pltpu.SemaphoreType.DMA((len(pieces),)),
        ],
        name="project",
    )(order, own, sib, *[p[2] for p in pieces])


def expert_kernel(count, share_ref, gate_ref, up_ref, down_ref, *rest):
    blocks, outs, (rows, total) = rest[:count], rest[count : 2 * count], rest[2 * count :]
    step = pl.program_id(0)
    size = blocks[0].shape[0]

    @pl.when(step == 0)
    def _():
        for i in range(count):
            rows[pl.ds(i * size, size), :] = blocks[i][...]

    gate = jnp.dot(rows[...], gate_ref[0], preferred_element_type=F32)
    up = jnp.dot(rows[...], up_ref[0], preferred_element_type=F32)
    hidden = (jax.nn.silu(gate) * up * share_ref[0]).astype(BF16)
    part = jnp.dot(hidden, down_ref[0], preferred_element_type=F32)

    @pl.when(step == 0)
    def _():
        total[...] = part

    @pl.when(step > 0)
    def _():
        total[...] += part

    @pl.when(step == pl.num_programs(0) - 1)
    def _():
        for i in range(count):
            outs[i][...] = total[pl.ds(i * size, size), :].astype(BF16)


def experts(share, gate, up, down, blocks):
    count = len(blocks)
    size, width = blocks[0].shape
    number, _, hid = gate.shape
    whole = pl.BlockSpec((size, width), lambda e: (0, 0))
    return pl.pallas_call(
        functools.partial(expert_kernel, count),
        grid=(number,),
        out_shape=[jax.ShapeDtypeStruct((size, width), BF16)] * count,
        in_specs=[
            pl.BlockSpec((1, count * size, 1), lambda e: (e, 0, 0)),
            pl.BlockSpec((1, width, hid), lambda e: (e, 0, 0)),
            pl.BlockSpec((1, width, hid), lambda e: (e, 0, 0)),
            pl.BlockSpec((1, hid, width), lambda e: (e, 0, 0)),
        ]
        + [whole] * count,
        out_specs=[whole] * count,
        scratch_shapes=[
            pltpu.VMEM((count * size, width), BF16),
            pltpu.VMEM((count * size, width), F32),
        ],
        name="experts",
    )(share, gate, up, down, *blocks)


def local(
    moves,
    ssd_x,
    ssd_z,
    ssd_b,
    ssd_c,
    dt_raw,
    dt_bias,
    a_log,
    d_skip,
    norm_gain,
    cache_state,
    cache_owner,
    resid,
    w_out,
    moe_gain,
    expert_ids,
    route_weight,
    expert_home,
    w_gate,
    w_up,
    w_down,
):
    devices = moves.count
    nz, ny, nx, _ = moves.sizes
    me = lax.axis_index("wide")
    core = me % 2
    chip = me // 2
    tok_dev = ssd_x.shape[0]
    heads_all = dt_raw.shape[1]
    columns = ssd_x.shape[1]
    per_dev = columns // devices
    head_dim = columns // heads_all
    state_size = ssd_b.shape[1]
    req_local = tok_dev // SEQ
    requests = cache_owner.shape[0]
    width = resid.shape[1]
    half_w, half_t = width // 2, tok_dev // 2

    place_z = chip // (ny * nx)
    place_y = (chip // nx) % ny
    place_x = chip % nx

    def back(kz, ky, kx):
        return (
            ((place_z + nz - kz) % nz) * ny + (place_y + ny - ky) % ny
        ) * nx + (place_x + nx - kx) % nx

    slots_local = cache_state.shape[0]
    state_view = cache_state.reshape(slots_local, devices, per_dev, state_size)
    by_heads = lax.all_to_all(state_view, "wide", split_axis=1, concat_axis=0, tiled=True)
    by_heads = by_heads.reshape(-1, per_dev, state_size)
    c_all = lax.all_to_all(
        jnp.broadcast_to(ssd_c[None], (devices,) + ssd_c.shape), "wide", 0, 0
    ).reshape(requests, SEQ, state_size)

    weight_f = route_weight.astype(F32)
    share = weight_f / jnp.sum(weight_f, axis=-1, keepdims=True)
    expert_count = expert_home.shape[0]
    own_experts = expert_count // devices
    lookup = expert_ids[..., None] == jnp.arange(expert_count, dtype=jnp.int32)
    target = jnp.sum(jnp.where(lookup, expert_home, 0), axis=-1)
    by_row = jnp.sum(
        jnp.where(
            jnp.arange(expert_count, dtype=jnp.int32)[:, None, None] == target[None],
            share[None],
            0.0,
        ),
        axis=-1,
    ).reshape(devices // 2, 2, own_experts, tok_dev)
    share_send = jnp.stack([by_row, by_row[:, ::-1]], axis=2)
    share_send = share_send.reshape(devices, 2 * own_experts, tok_dev)
    share_all = lax.all_to_all(share_send, "wide", 0, 0)
    share_all = share_all.reshape(devices // 2, 2, 2 * own_experts, tok_dev)
    share_core = lax.dynamic_index_in_dim(share_all, core, 1, keepdims=False)

    both = lambda w: jnp.concatenate([w, moves.turn(w, CORE)], axis=0)
    gate2, up2, down2 = both(w_gate), both(w_up), both(w_down)

    left = moves.gather(w_out[:, :half_w], X, Y)
    right = moves.gather(w_out[:, half_w:], Y, X)
    pieces, order = [], []
    for kz in range(nz):
        for ky in range(ny):
            for kx in range(nx):
                slot = len(order)
                order.append(back(kz, ky, kx))
                pieces.append((slot, 0, left[kz][kx][ky]))
                pieces.append((slot, half_w, right[kz][ky][kx]))
    order = jnp.stack(order)

    rates = -jnp.exp(a_log)
    local_step, local_cum = head_steps(dt_raw, dt_bias, rates, req_local)
    intra = intra_terms(
        ssd_x.reshape(req_local, SEQ, heads_all, head_dim),
        local_step,
        local_cum,
        ssd_b.reshape(req_local, SEQ, state_size),
        ssd_c.reshape(req_local, SEQ, state_size),
        d_skip,
    )

    def block_major(a):
        return jnp.swapaxes(a.reshape(tok_dev, devices, per_dev), 0, 1)

    intra_bm = block_major(intra.reshape(tok_dev, columns))
    z_bm = block_major(ssd_z)
    grow = jnp.repeat(jnp.exp(local_cum).reshape(tok_dev, heads_all), head_dim, axis=1)
    grow_bm = block_major(grow)

    product = carried_terms(cache_owner, c_all, by_heads)
    product = product.reshape(devices, tok_dev, per_dev)
    carried = lax.all_to_all(product, "wide", 0, 0)
    mixed = intra_bm.astype(F32) + carried.astype(F32) * grow_bm
    gated = mixed * jax.nn.silu(z_bm.astype(F32))
    scale = lax.rsqrt(jnp.sum(gated * gated, axis=(0, 2), keepdims=True) / columns + 1e-05)
    ssd_bm = (gated * scale * norm_gain.reshape(devices, 1, per_dev)).astype(BF16)
    ssd_out = jnp.swapaxes(ssd_bm, 0, 1).reshape(tok_dev, columns)

    by_core = ssd_bm.reshape(devices // 2, 2, tok_dev, per_dev)
    mine = lax.dynamic_index_in_dim(by_core, core, 1, keepdims=False)
    other = lax.dynamic_index_in_dim(by_core, 1 - core, 1, keepdims=False)
    own_part, sib_part = project(order, mine, moves.turn(other, CORE), pieces)
    wide_moe = resid.astype(F32) + own_part + moves.turn(sib_part, CORE)
    normed = (
        wide_moe
        * lax.rsqrt(jnp.mean(wide_moe * wide_moe, axis=-1, keepdims=True) + 1e-05)
        * moe_gain
    ).astype(BF16)

    top = moves.gather(normed[:half_t], X, Y)
    low = moves.gather(normed[half_t:], Y, X)
    top_z, low_z = [], []
    for kz in range(nz):
        blocks = [b for row in top[kz] for b in row] + [b for row in low[kz] for b in row]
        at_top = [back(kz, ky, kx) for kx in range(nx) for ky in range(ny)]
        at_low = [back(kz, ky, kx) for ky in range(ny) for kx in range(nx)]
        shares = jnp.concatenate(
            [share_core[i][:, :half_t] for i in at_top]
            + [share_core[i][:, half_t:] for i in at_low],
            axis=1,
        )[..., None]
        outs = experts(shares, gate2, up2, down2, blocks)
        n = ny * nx
        top_rows = [outs[i * ny : (i + 1) * ny] for i in range(nx)]
        low_rows = [outs[n + i * nx : n + (i + 1) * nx] for i in range(ny)]
        top_z.append(moves.plane_fold(top_rows, X, Y))
        low_z.append(moves.plane_fold(low_rows, Y, X))
    moe_out = jnp.concatenate([moves.fold(top_z, Z), moves.fold(low_z, Z)], axis=0).astype(BF16)
    return (ssd_out, moe_out)


def solution(mesh):
    both = ("group", "wide")
    in_specs = (
        P(both, None),
        P(both, None),
        P(both, None),
        P(both, None),
        P(both, None),
        P(),
        P(),
        P(),
        P(),
        P(both, None, None, None),
        P("group"),
        P(both, None),
        P("wide", None),
        P(),
        P(both, None),
        P(both, None),
        P(),
        P("wide", None, None),
        P("wide", None, None),
        P("wide", None, None),
    )
    out_specs = (P(both, None), P(both, None))
    step = functools.partial(local, Moves(grid_of(mesh)))
    return jax.shard_map(step, mesh=mesh, in_specs=in_specs, out_specs=out_specs, check_vma=False)
```

```python
import functools

import jax
import jax.numpy as jnp
import numpy as np
from jax import lax
from jax.experimental import pallas as pl
from jax.experimental.pallas import tpu as pltpu
from jax.sharding import PartitionSpec as P

SEQ = 32
EARLY = 2

F32, BF16 = jnp.float32, jnp.bfloat16
Z, Y, X, CORE = 0, 1, 2, 3


def grid_of(mesh):
    wide = mesh.shape["wide"]
    line = np.asarray(mesh.devices).reshape(-1, wide)[0]
    try:
        places = [(d.coords[2], d.coords[1], d.coords[0], d.core_on_chip) for d in line]
    except (AttributeError, TypeError, IndexError):
        return (wide // 2, 1, 1, 2)
    ticks = [sorted({p[a] for p in places}) for a in range(4)]
    sizes = tuple(len(t) for t in ticks)
    ranks = [tuple(ticks[a].index(p[a]) for a in range(4)) for p in places]
    plane = sizes[Y] <= 2 and sizes[X] <= 2 and sizes[CORE] == 2
    if plane and int(np.prod(sizes)) == wide and ranks == list(np.ndindex(*sizes)):
        return sizes
    return (wide // 2, 1, 1, 2)


class Moves:
    def __init__(self, sizes):
        self.sizes = sizes
        self.count = int(np.prod(sizes))
        self.forward = sizes[Z] // 2
        self.z_steps = list(range(sizes[Z]))

    def turn(self, value, axis, step=1):
        pairs = []
        for i, place in enumerate(np.ndindex(*self.sizes)):
            to = list(place)
            to[axis] = (to[axis] + step) % self.sizes[axis]
            pairs.append((i, int(np.ravel_multi_index(to, self.sizes))))
        return lax.ppermute(value, "wide", pairs)

    def doubled(self, value, axis):
        if self.sizes[axis] == 1:
            return value
        return jnp.concatenate([value, self.turn(value, axis)], axis=0)

    def z_ring(self, value):
        size = self.sizes[Z]
        held = {0: value}
        for k in range(1, self.forward + 1):
            held[k] = self.turn(held[k - 1], Z)
        for k in range(size - 1, self.forward, -1):
            held[k] = self.turn(held[(k + 1) % size], Z, -1)
        return [held[k] for k in range(size)]

    def z_fold(self, parts):
        size = self.sizes[Z]
        total = parts[0].astype(F32)
        ahead = None
        for k in range(self.forward, 0, -1):
            ahead = parts[k] if ahead is None else parts[k].astype(F32) + ahead.astype(F32)
            ahead = self.turn(ahead.astype(BF16), Z, -1)
        behind = None
        for k in range(self.forward + 1, size):
            behind = parts[k] if behind is None else parts[k].astype(F32) + behind.astype(F32)
            behind = self.turn(behind.astype(BF16), Z)
        for part in (ahead, behind):
            if part is not None:
                total = total + part.astype(F32)
        return total

    def axes(self, kz):
        return (X, Y) if kz % 2 == 0 else (Y, X)

    def offsets(self, kz):
        first, second = self.axes(kz)
        out = []
        for s in range(self.sizes[second]):
            for f in range(self.sizes[first]):
                out.append((f, s) if first == Y else (s, f))
        return out

    def plane(self, value, kz):
        first, second = self.axes(kz)
        near = self.doubled(value, first)
        if self.sizes[second] == 1:
            return [near]
        return [near, self.turn(near, second)]

    def plane_fold(self, parts, kz):
        first, second = self.axes(kz)
        total = parts[0].astype(F32)
        if self.sizes[second] > 1:
            total = total + self.turn(parts[1], second).astype(F32)
        if self.sizes[first] > 1:
            rows = total.shape[0] // 2
            far = self.turn(total[rows:].astype(BF16), first)
            total = total[:rows] + far.astype(F32)
        return total


def intra_terms(inputs, step_size, cumulative, b_proj, c_proj, skip_gain):
    scores = jnp.einsum("rtn,rsn->rts", c_proj, b_proj, preferred_element_type=F32)
    length = inputs.shape[1]
    causal = jnp.arange(length)[:, None] >= jnp.arange(length)[None, :]
    cum_heads = jnp.swapaxes(cumulative, 1, 2)
    log_gap = cum_heads[..., :, None] - cum_heads[..., None, :]
    decays = jnp.where(causal, jnp.exp(jnp.where(causal, log_gap, 0.0)), 0.0)
    mixing = (scores[:, None] * decays * jnp.swapaxes(step_size, 1, 2)[:, :, None, :]).astype(BF16)
    result = jnp.einsum("rhts,rshp->rthp", mixing, inputs, preferred_element_type=F32)
    result = result + skip_gain[None, None, :, None] * inputs.astype(F32)
    return result.astype(BF16)


def head_steps(raw_steps, bias_part, rate_part, requests):
    step_size = jax.nn.softplus(raw_steps.astype(F32) + bias_part)
    step_size = step_size.reshape(requests, SEQ, step_size.shape[-1])
    return (step_size, jnp.cumsum(step_size * rate_part, axis=1))


def carried_kernel(owner, order, c_ref, state_ref, out_ref):
    per_dev = c_ref.shape[1]

    def one(s, carry):
        d = order[s]
        for i in range(per_dev):
            out_ref[d * per_dev + i] = lax.dot_general(
                c_ref[s, i],
                state_ref[owner[d * per_dev + i]],
                (((1,), (1,)), ((), ())),
                preferred_element_type=F32,
            ).astype(BF16)
        return carry

    lax.fori_loop(0, c_ref.shape[0], one, 0, unroll=4)


def carried_terms(owner, order, c_rel, states):
    devices, per_dev, length, _ = c_rel.shape
    vmem, smem = pl.BlockSpec(memory_space=pltpu.VMEM), pl.BlockSpec(memory_space=pltpu.SMEM)
    return pl.pallas_call(
        carried_kernel,
        out_shape=jax.ShapeDtypeStruct((devices * per_dev, length, states.shape[1]), BF16),
        in_specs=[smem, smem, vmem, vmem],
        out_specs=vmem,
        name="carried",
    )(owner, order, c_rel, states)


def project_kernel(order, own_ref, sib_ref, *rest):
    pieces, (own_out, sib_out, weight, rows, sems) = rest[:-5], rest[-5:]
    depth = own_ref.shape[2]
    half = own_ref.shape[1]
    copies, at = [], 0
    for i, piece in enumerate(pieces):
        copies.append(
            pltpu.make_async_copy(piece, weight.at[pl.ds(at, piece.shape[0])], sems.at[i])
        )
        copies[-1].start()
        at += piece.shape[0]
    for s in range(order.shape[0]):
        rows[pl.ds(0, half), pl.ds(s * depth, depth)] = own_ref[order[s]]
        rows[pl.ds(half, half), pl.ds(s * depth, depth)] = sib_ref[order[s]]
    total, at = None, 0
    for piece, copy in zip(pieces, copies):
        copy.wait()
        span = pl.ds(at, piece.shape[0])
        part = jnp.dot(rows[:, span], weight[span, :], preferred_element_type=F32)
        total = part if total is None else total + part
        at += piece.shape[0]
    own_out[...] = total[:half]
    sib_out[...] = total[half:]


def project(order, own, sib, pieces):
    chips, tokens, depth = own.shape
    width = pieces[0].shape[1]
    vmem = pl.BlockSpec(memory_space=pltpu.VMEM)
    return pl.pallas_call(
        project_kernel,
        out_shape=(
            jax.ShapeDtypeStruct((tokens, width), F32),
            jax.ShapeDtypeStruct((tokens, width), F32),
        ),
        in_specs=[pl.BlockSpec(memory_space=pltpu.SMEM), vmem, vmem]
        + [pl.BlockSpec(memory_space=pl.ANY)] * len(pieces),
        out_specs=(vmem, vmem),
        scratch_shapes=[
            pltpu.VMEM((chips * depth, width), BF16),
            pltpu.VMEM((2 * tokens, chips * depth), BF16),
            pltpu.SemaphoreType.DMA((len(pieces),)),
        ],
        name="project",
    )(order, own, sib, *pieces)


def expert_kernel(count, number, spread, mine, share_ref, *rest):
    weights, blocks = rest[: 3 * number], rest[3 * number : 3 * number + count]
    outs = rest[3 * number + count : 3 * number + 2 * count]
    gate_s, up_s, down_s, rows, hidden, result, w_sems, r_sems, o_sems = rest[
        3 * number + 2 * count :
    ]
    hid = gate_s.shape[2]
    copies, at = [], 0
    for i, block in enumerate(blocks):
        copies.append(
            pltpu.make_async_copy(block, rows.at[pl.ds(at, block.shape[0])], r_sems.at[i])
        )
        copies[-1].start()
        at += block.shape[0]
    loads = []
    for e in range(number):
        gate, up, down = weights[3 * e : 3 * e + 3]
        loads.append(
            [
                pltpu.make_async_copy(gate, gate_s.at[e], w_sems.at[3 * e]),
                pltpu.make_async_copy(up, up_s.at[e], w_sems.at[3 * e + 1]),
                pltpu.make_async_copy(
                    down, down_s.at[pl.ds(e * hid, hid)], w_sems.at[3 * e + 2]
                ),
            ]
        )
    for e in range(number):
        loads[e][0].start()
        loads[e][1].start()
    for e in range(number):
        loads[e][2].start()
    for copy in copies:
        copy.wait()
    lane = lax.broadcasted_iota(jnp.int32, share_ref.shape, 1)
    for e in range(number):
        here = (lane == mine[e]) | (lane == mine[e] + spread)
        share = jnp.sum(jnp.where(here, share_ref[...].astype(F32), 0.0), axis=1, keepdims=True)
        loads[e][0].wait()
        gate = jnp.dot(rows[...], gate_s[e], preferred_element_type=F32)
        loads[e][1].wait()
        up = jnp.dot(rows[...], up_s[e], preferred_element_type=F32)
        hidden[:, pl.ds(e * hid, hid)] = (jax.nn.silu(gate) * up * share).astype(BF16)
    for e in range(number):
        loads[e][2].wait()
    width = result.shape[1]
    parts = 4 if width % 512 == 0 else 1
    stores = []
    for c in range(parts):
        span = pl.ds(c * (width // parts), width // parts)
        result[:, span] = jnp.dot(
            hidden[...], down_s[:, span], preferred_element_type=F32
        ).astype(BF16)
        at = 0
        for i, out in enumerate(outs):
            stores.append(
                pltpu.make_async_copy(
                    result.at[pl.ds(at, out.shape[0]), span],
                    out.at[:, span],
                    o_sems.at[i * parts + c],
                )
            )
            stores[-1].start()
            at += out.shape[0]
    for store in stores:
        store.wait()


def experts(mine, share, weights, blocks, spread):
    count, number = len(blocks), len(weights) // 3
    width, hid = weights[0].shape
    total = sum(b.shape[0] for b in blocks)
    hbm = pl.BlockSpec(memory_space=pl.ANY)
    parts = 4 if width % 512 == 0 else 1
    return pl.pallas_call(
        functools.partial(expert_kernel, count, number, spread),
        out_shape=[jax.ShapeDtypeStruct(b.shape, BF16) for b in blocks],
        in_specs=[
            pl.BlockSpec(memory_space=pltpu.SMEM),
            pl.BlockSpec(memory_space=pltpu.VMEM),
        ]
        + [hbm] * (3 * number + count),
        out_specs=[hbm] * count,
        scratch_shapes=[
            pltpu.VMEM((number, width, hid), BF16),
            pltpu.VMEM((number, width, hid), BF16),
            pltpu.VMEM((number * hid, width), BF16),
            pltpu.VMEM((total, width), BF16),
            pltpu.VMEM((total, number * hid), BF16),
            pltpu.VMEM((total, width), BF16),
            pltpu.SemaphoreType.DMA((3 * number,)),
            pltpu.SemaphoreType.DMA((count,)),
            pltpu.SemaphoreType.DMA((count * parts,)),
        ],
        name="experts",
    )(mine, share, *weights, *blocks)


def local(
    moves,
    ssd_x,
    ssd_z,
    ssd_b,
    ssd_c,
    dt_raw,
    dt_bias,
    a_log,
    d_skip,
    norm_gain,
    cache_state,
    cache_owner,
    resid,
    w_out,
    moe_gain,
    expert_ids,
    route_weight,
    expert_home,
    w_gate,
    w_up,
    w_down,
):
    devices = moves.count
    nz, ny, nx, _ = moves.sizes
    me = lax.axis_index("wide")
    core = me % 2
    chip = me // 2
    tok_dev = ssd_x.shape[0]
    heads_all = dt_raw.shape[1]
    columns = ssd_x.shape[1]
    per_dev = columns // devices
    head_dim = columns // heads_all
    state_size = ssd_b.shape[1]
    req_local = tok_dev // SEQ
    width = resid.shape[1]
    place_z = chip // (ny * nx)
    place_y = (chip // nx) % ny
    place_x = chip % nx

    def back(kz, ky, kx):
        row = ((place_z + nz - kz) % nz) * ny + (place_y + ny - ky) % ny
        return row * nx + (place_x + nx - kx) % nx

    slots_local = cache_state.shape[0]
    state_view = cache_state.reshape(slots_local, devices, per_dev, state_size)
    by_heads = lax.all_to_all(state_view, "wide", split_axis=1, concat_axis=0, tiled=True)
    by_heads = by_heads.reshape(-1, per_dev, state_size)

    weight_f = route_weight.astype(F32)
    share = weight_f / jnp.sum(weight_f, axis=-1, keepdims=True)
    expert_count = expert_home.shape[0]
    own_experts = expert_count // devices
    lookup = expert_ids[..., None] == jnp.arange(expert_count, dtype=jnp.int32)
    target = jnp.sum(jnp.where(lookup, expert_home, 0), axis=-1)
    by_row = jnp.sum(
        jnp.where(
            target[..., None] == jnp.arange(expert_count, dtype=jnp.int32), share[..., None], 0.0
        ),
        axis=1,
    )
    coarse = by_row.astype(BF16)
    fine = (by_row - coarse.astype(F32)).astype(BF16)
    known = jnp.concatenate([ssd_c, coarse, fine], axis=1)
    known = jnp.pad(known, ((0, 0), (0, -known.shape[1] % 128)))[None]
    known = moves.doubled(moves.doubled(moves.doubled(known, CORE), X), Y)
    known = moves.z_ring(known)
    near = jnp.arange(ny * nx * 2, dtype=jnp.int32)
    rel_order = jnp.concatenate(
        [
            back(kz, near // (2 * nx), (near // 2) % nx) * 2 + (core + near) % 2
            for kz in range(nz)
        ]
    )
    c_rel = jnp.concatenate([k[..., :state_size] for k in known], axis=0)
    c_rel = c_rel.reshape(devices, req_local, SEQ, state_size)
    shares = [
        jnp.concatenate(
            [known[kz][2 * (ky * nx + kx), :, state_size:] for ky, kx in moves.offsets(kz)], axis=0
        )
        for kz in range(nz)
    ]

    weights = []
    for swap in (False, True):
        for e in range(own_experts):
            weights += [moves.turn(w[e], CORE) if swap else w[e] for w in (w_gate, w_up, w_down)]
    near_lane = jnp.arange(own_experts, dtype=jnp.int32)
    lanes = jnp.concatenate(
        [me * own_experts + near_lane, (me + 1 - 2 * core) * own_experts + near_lane]
    )

    w_rows = [moves.plane(a, kz) for kz, a in enumerate(moves.z_ring(w_out))]
    order = jnp.stack([back(kz, ky, kx) for kz in range(nz) for ky, kx in moves.offsets(kz)])

    rates = -jnp.exp(a_log)
    local_step, local_cum = head_steps(dt_raw, dt_bias, rates, req_local)
    intra = intra_terms(
        ssd_x.reshape(req_local, SEQ, heads_all, head_dim),
        local_step,
        local_cum,
        ssd_b.reshape(req_local, SEQ, state_size),
        ssd_c.reshape(req_local, SEQ, state_size),
        d_skip,
    )

    def block_major(a):
        return jnp.swapaxes(a.reshape(tok_dev, devices, per_dev), 0, 1)

    intra_bm = block_major(intra.reshape(tok_dev, columns))
    z_bm = block_major(ssd_z)
    grow = jnp.repeat(jnp.exp(local_cum).reshape(tok_dev, heads_all), head_dim, axis=1)
    grow_bm = block_major(grow)

    early, late = w_rows[:EARLY], w_rows[EARLY:]
    by_heads, early, weights, shares, intra_bm, z_bm, grow_bm = lax.optimization_barrier(
        (by_heads, early, weights, shares, intra_bm, z_bm, grow_bm)
    )
    product = carried_terms(cache_owner, rel_order, c_rel, by_heads)
    product = product.reshape(devices, tok_dev, per_dev)
    carried = lax.all_to_all(product, "wide", 0, 0)
    mixed = intra_bm.astype(F32) + carried.astype(F32) * grow_bm
    gated = mixed * jax.nn.silu(z_bm.astype(F32))
    scale = lax.rsqrt(jnp.sum(gated * gated, axis=(0, 2), keepdims=True) / columns + 1e-05)
    ssd_bm = (gated * scale * norm_gain.reshape(devices, 1, per_dev)).astype(BF16)
    ssd_out = jnp.swapaxes(ssd_bm, 0, 1).reshape(tok_dev, columns)

    by_core = ssd_bm.reshape(devices // 2, 2, tok_dev, per_dev)
    mine = lax.dynamic_index_in_dim(by_core, core, 1, keepdims=False)
    other = lax.dynamic_index_in_dim(by_core, 1 - core, 1, keepdims=False)
    own_part, sib_part = project(order, mine, moves.turn(other, CORE), sum(early + late, []))
    wide_moe = resid.astype(F32) + own_part + moves.turn(sib_part, CORE)
    normed = (
        wide_moe
        * lax.rsqrt(jnp.mean(wide_moe * wide_moe, axis=-1, keepdims=True) + 1e-05)
        * moe_gain
    ).astype(BF16)

    held = moves.z_ring(normed)
    parts = [None] * nz
    for group in [moves.z_steps[i : i + 2] for i in range(0, nz, 2)]:
        blocks = [moves.plane(held[kz], kz) for kz in group]
        share_rows = jnp.concatenate([shares[kz] for kz in group], axis=0)
        outs = experts(lanes, share_rows, weights, sum(blocks, []), expert_count)
        for kz, b in zip(group, blocks):
            parts[kz] = moves.plane_fold(outs[: len(b)], kz)
            outs = outs[len(b) :]
    moe_out = moves.z_fold(parts).astype(BF16)
    return (ssd_out, moe_out)


def solution(mesh):
    both = ("group", "wide")
    in_specs = (
        P(both, None),
        P(both, None),
        P(both, None),
        P(both, None),
        P(both, None),
        P(),
        P(),
        P(),
        P(),
        P(both, None, None, None),
        P("group"),
        P(both, None),
        P("wide", None),
        P(),
        P(both, None),
        P(both, None),
        P(),
        P("wide", None, None),
        P("wide", None, None),
        P("wide", None, None),
    )
    out_specs = (P(both, None), P(both, None))
    step = functools.partial(local, Moves(grid_of(mesh)))
    return jax.shard_map(step, mesh=mesh, in_specs=in_specs, out_specs=out_specs, check_vma=False)
```

```python
import functools

import jax
import jax.numpy as jnp
import numpy as np
from jax import lax
from jax.experimental import pallas as pl
from jax.experimental.pallas import tpu as pltpu
from jax.sharding import PartitionSpec as P

SEQ = 32

F32, BF16 = jnp.float32, jnp.bfloat16
Z, Y, X, CORE = 0, 1, 2, 3


def grid_of(mesh):
    wide = mesh.shape["wide"]
    line = np.asarray(mesh.devices).reshape(-1, wide)[0]
    try:
        places = [(d.coords[2], d.coords[1], d.coords[0], d.core_on_chip) for d in line]
    except (AttributeError, TypeError, IndexError):
        return (wide // 2, 1, 1, 2)
    ticks = [sorted({p[a] for p in places}) for a in range(4)]
    sizes = tuple(len(t) for t in ticks)
    ranks = [tuple(ticks[a].index(p[a]) for a in range(4)) for p in places]
    plane = sizes[Y] <= 2 and sizes[X] <= 2 and sizes[CORE] == 2
    if plane and int(np.prod(sizes)) == wide and ranks == list(np.ndindex(*sizes)):
        return sizes
    return (wide // 2, 1, 1, 2)


class Moves:
    def __init__(self, sizes):
        self.sizes = sizes
        self.count = int(np.prod(sizes))
        self.forward = sizes[Z] // 2
        self.z_steps = list(range(sizes[Z]))

    def turn(self, value, axis, step=1):
        pairs = []
        for i, place in enumerate(np.ndindex(*self.sizes)):
            to = list(place)
            to[axis] = (to[axis] + step) % self.sizes[axis]
            pairs.append((i, int(np.ravel_multi_index(to, self.sizes))))
        return lax.ppermute(value, "wide", pairs)

    def doubled(self, value, axis):
        if self.sizes[axis] == 1:
            return value
        return jnp.concatenate([value, self.turn(value, axis)], axis=0)

    def z_ring(self, value):
        size = self.sizes[Z]
        held = {0: value}
        for k in range(1, self.forward + 1):
            held[k] = self.turn(held[k - 1], Z)
        for k in range(size - 1, self.forward, -1):
            held[k] = self.turn(held[(k + 1) % size], Z, -1)
        return [held[k] for k in range(size)]

    def z_fold(self, parts):
        size = self.sizes[Z]
        total = parts[0].astype(F32)
        ahead = None
        for k in range(self.forward, 0, -1):
            ahead = parts[k] if ahead is None else parts[k].astype(F32) + ahead.astype(F32)
            ahead = self.turn(ahead.astype(BF16), Z, -1)
        behind = None
        for k in range(self.forward + 1, size):
            behind = parts[k] if behind is None else parts[k].astype(F32) + behind.astype(F32)
            behind = self.turn(behind.astype(BF16), Z)
        for part in (ahead, behind):
            if part is not None:
                total = total + part.astype(F32)
        return total

    def axes(self, kz):
        return (X, Y) if kz % 2 == 0 else (Y, X)

    def offsets(self, kz):
        first, second = self.axes(kz)
        out = []
        for s in range(self.sizes[second]):
            for f in range(self.sizes[first]):
                out.append((f, s) if first == Y else (s, f))
        return out

    def plane(self, value, kz):
        first, second = self.axes(kz)
        near = self.doubled(value, first)
        if self.sizes[second] == 1:
            return [near]
        return [near, self.turn(near, second)]

    def plane_fold(self, parts, kz):
        first, second = self.axes(kz)
        total = parts[0].astype(F32)
        if self.sizes[second] > 1:
            total = total + self.turn(parts[1], second).astype(F32)
        if self.sizes[first] > 1:
            rows = total.shape[0] // 2
            far = self.turn(total[rows:].astype(BF16), first)
            total = total[:rows] + far.astype(F32)
        return total


def intra_terms(inputs, step_size, cumulative, b_proj, c_proj, skip_gain):
    scores = jnp.einsum("rtn,rsn->rts", c_proj, b_proj, preferred_element_type=F32)
    length = inputs.shape[1]
    causal = jnp.arange(length)[:, None] >= jnp.arange(length)[None, :]
    cum_heads = jnp.swapaxes(cumulative, 1, 2)
    log_gap = cum_heads[..., :, None] - cum_heads[..., None, :]
    decays = jnp.where(causal, jnp.exp(jnp.where(causal, log_gap, 0.0)), 0.0)
    mixing = (scores[:, None] * decays * jnp.swapaxes(step_size, 1, 2)[:, :, None, :]).astype(BF16)
    result = jnp.einsum("rhts,rshp->rthp", mixing, inputs, preferred_element_type=F32)
    result = result + skip_gain[None, None, :, None] * inputs.astype(F32)
    return result.astype(BF16)


def head_steps(raw_steps, bias_part, rate_part, requests):
    step_size = jax.nn.softplus(raw_steps.astype(F32) + bias_part)
    step_size = step_size.reshape(requests, SEQ, step_size.shape[-1])
    return (step_size, jnp.cumsum(step_size * rate_part, axis=1))


def carried_kernel(owner, order, place, c_ref, state_ref, out_ref):
    per_dev = c_ref.shape[1]

    def one(s, carry):
        d, p = order[s], place[s]
        for i in range(per_dev):
            out_ref[p * per_dev + i] = lax.dot_general(
                c_ref[s, i],
                state_ref[owner[d * per_dev + i]],
                (((1,), (1,)), ((), ())),
                preferred_element_type=F32,
            ).astype(BF16)
        return carry

    lax.fori_loop(0, c_ref.shape[0], one, 0, unroll=4)


def carried_terms(owner, order, place, c_rel, states):
    devices, per_dev, length, n = c_rel.shape
    cols = states.shape[1]
    vmem, smem = pl.BlockSpec(memory_space=pltpu.VMEM), pl.BlockSpec(memory_space=pltpu.SMEM)
    cost = pl.CostEstimate(
        flops=2 * devices * per_dev * length * n * cols,
        transcendentals=0,
        bytes_accessed=2 * (states.size + c_rel.size + devices * per_dev * length * cols),
    )
    return pl.pallas_call(
        carried_kernel,
        out_shape=jax.ShapeDtypeStruct((devices * per_dev, length, cols), BF16),
        in_specs=[smem, smem, smem, vmem, vmem],
        out_specs=vmem,
        cost_estimate=cost,
        name="carried",
    )(owner, order, place, c_rel, states)


def mixer_kernel(steps, order, carried_ref, grow_ref, gain_ref, *rest):
    terms, rest = rest[:steps], rest[steps:]
    weight, rows, sems = rest[-3:]
    count = sems.shape[0]
    pieces, outs = rest[:count], rest[count:-3]
    gated_outs, square_out, own_out, far_outs = (
        outs[:steps],
        outs[steps],
        outs[steps + 1],
        outs[steps + 2 :],
    )
    copies, at = [], 0
    for i, piece in enumerate(pieces):
        copies.append(
            pltpu.make_async_copy(piece, weight.at[pl.ds(at, piece.shape[0])], sems.at[i])
        )
        copies[-1].start()
        at += piece.shape[0]
    tokens, depth = terms[0].shape[2:]
    for k in range(steps):
        span = pl.ds(k * tokens, tokens)
        square = None
        for s in range(order.shape[0]):
            b = order[s]
            grown = carried_ref[b, span, :].astype(F32) * grow_ref[b, span, :]
            gate = terms[k][1, b].astype(F32)
            gated = (terms[k][0, b].astype(F32) + grown) * jax.nn.silu(gate)
            square = gated * gated if square is None else square + gated * gated
            scaled = (gated * gain_ref[b]).astype(BF16)
            rows[span, pl.ds(s * depth, depth)] = scaled
            gated_outs[k][b] = scaled
        square_out[k] = square
    total, at = None, 0
    for piece, copy in zip(pieces, copies):
        copy.wait()
        span = pl.ds(at, piece.shape[0])
        part = jnp.dot(rows[:, span], weight[span, :], preferred_element_type=F32)
        total = part if total is None else total + part
        at += piece.shape[0]
    own_out[...] = total[:tokens]
    for k in range(1, steps):
        far_outs[k - 1][...] = total[k * tokens : (k + 1) * tokens].astype(BF16)


def mixer(order, carried, grow, gain, terms, pieces):
    steps, count = len(terms), len(pieces)
    _, blocks, tokens, depth = terms[0].shape
    width = pieces[0].shape[1]
    vmem, hbm = pl.BlockSpec(memory_space=pltpu.VMEM), pl.BlockSpec(memory_space=pl.ANY)
    shape = jax.ShapeDtypeStruct
    cost = pl.CostEstimate(
        flops=2 * steps * tokens * blocks * depth * width,
        transcendentals=steps * tokens * blocks * depth,
        bytes_accessed=2 * blocks * depth * width + 12 * carried.size,
    )
    outs = pl.pallas_call(
        functools.partial(mixer_kernel, steps),
        out_shape=[shape((blocks, tokens, depth), BF16)] * steps
        + [shape((steps, tokens, depth), F32), shape((tokens, width), F32)]
        + [shape((tokens, width), BF16)] * (steps - 1),
        in_specs=[pl.BlockSpec(memory_space=pltpu.SMEM)] + [vmem] * (3 + steps) + [hbm] * count,
        out_specs=[vmem] * (2 * steps + 1),
        scratch_shapes=[
            pltpu.VMEM((blocks * depth, width), BF16),
            pltpu.VMEM((steps * tokens, blocks * depth), BF16),
            pltpu.SemaphoreType.DMA((count,)),
        ],
        cost_estimate=cost,
        name="mixer",
    )(order, carried, grow, gain, *terms, *pieces)
    return outs[:steps], outs[steps], outs[steps + 1 :]


def expert_kernel(count, number, spread, mine, share_ref, *rest):
    weights, blocks = rest[: 3 * number], rest[3 * number : 3 * number + count]
    outs = rest[3 * number + count : 3 * number + 2 * count]
    gate_s, up_s, down_s, rows, hidden, result, w_sems, r_sems, o_sems = rest[
        3 * number + 2 * count :
    ]
    hid = gate_s.shape[2]
    copies, at = [], 0
    for i, block in enumerate(blocks):
        copies.append(
            pltpu.make_async_copy(block, rows.at[pl.ds(at, block.shape[0])], r_sems.at[i])
        )
        copies[-1].start()
        at += block.shape[0]
    loads = []
    for e in range(number):
        gate, up, down = weights[3 * e : 3 * e + 3]
        loads.append(
            [
                pltpu.make_async_copy(gate, gate_s.at[e], w_sems.at[3 * e]),
                pltpu.make_async_copy(up, up_s.at[e], w_sems.at[3 * e + 1]),
                pltpu.make_async_copy(
                    down, down_s.at[pl.ds(e * hid, hid)], w_sems.at[3 * e + 2]
                ),
            ]
        )
    for e in range(number):
        loads[e][0].start()
        loads[e][1].start()
    for e in range(number):
        loads[e][2].start()
    for copy in copies:
        copy.wait()
    lane = lax.broadcasted_iota(jnp.int32, share_ref.shape, 1)
    for e in range(number):
        here = (lane == mine[e]) | (lane == mine[e] + spread)
        share = jnp.sum(jnp.where(here, share_ref[...].astype(F32), 0.0), axis=1, keepdims=True)
        loads[e][0].wait()
        gate = jnp.dot(rows[...], gate_s[e], preferred_element_type=F32)
        loads[e][1].wait()
        up = jnp.dot(rows[...], up_s[e], preferred_element_type=F32)
        hidden[:, pl.ds(e * hid, hid)] = (jax.nn.silu(gate) * up * share).astype(BF16)
    for e in range(number):
        loads[e][2].wait()
    width = result.shape[1]
    parts = 4 if width % 512 == 0 else 1
    stores = []
    for c in range(parts):
        span = pl.ds(c * (width // parts), width // parts)
        result[:, span] = jnp.dot(
            hidden[...], down_s[:, span], preferred_element_type=F32
        ).astype(BF16)
        at = 0
        for i, out in enumerate(outs):
            stores.append(
                pltpu.make_async_copy(
                    result.at[pl.ds(at, out.shape[0]), span],
                    out.at[:, span],
                    o_sems.at[i * parts + c],
                )
            )
            stores[-1].start()
            at += out.shape[0]
    for store in stores:
        store.wait()


def experts(mine, share, weights, blocks, spread):
    count, number = len(blocks), len(weights) // 3
    width, hid = weights[0].shape
    total = sum(b.shape[0] for b in blocks)
    hbm = pl.BlockSpec(memory_space=pl.ANY)
    parts = 4 if width % 512 == 0 else 1
    return pl.pallas_call(
        functools.partial(expert_kernel, count, number, spread),
        out_shape=[jax.ShapeDtypeStruct(b.shape, BF16) for b in blocks],
        in_specs=[
            pl.BlockSpec(memory_space=pltpu.SMEM),
            pl.BlockSpec(memory_space=pltpu.VMEM),
        ]
        + [hbm] * (3 * number + count),
        out_specs=[hbm] * count,
        scratch_shapes=[
            pltpu.VMEM((number, width, hid), BF16),
            pltpu.VMEM((number, width, hid), BF16),
            pltpu.VMEM((number * hid, width), BF16),
            pltpu.VMEM((total, width), BF16),
            pltpu.VMEM((total, number * hid), BF16),
            pltpu.VMEM((total, width), BF16),
            pltpu.SemaphoreType.DMA((3 * number,)),
            pltpu.SemaphoreType.DMA((count,)),
            pltpu.SemaphoreType.DMA((count * parts,)),
        ],
        cost_estimate=pl.CostEstimate(
            flops=6 * total * width * hid * number,
            transcendentals=total * hid * number,
            bytes_accessed=2 * width * (3 * hid * number + 2 * total),
        ),
        name="experts",
    )(mine, share, *weights, *blocks)


def local(
    moves,
    ssd_x,
    ssd_z,
    ssd_b,
    ssd_c,
    dt_raw,
    dt_bias,
    a_log,
    d_skip,
    norm_gain,
    cache_state,
    cache_owner,
    resid,
    w_out,
    moe_gain,
    expert_ids,
    route_weight,
    expert_home,
    w_gate,
    w_up,
    w_down,
):
    devices = moves.count
    nz, ny, nx, _ = moves.sizes
    me = lax.axis_index("wide")
    core = me % 2
    chip = me // 2
    tok_dev = ssd_x.shape[0]
    heads_all = dt_raw.shape[1]
    columns = ssd_x.shape[1]
    per_dev = columns // devices
    head_dim = columns // heads_all
    state_size = ssd_b.shape[1]
    req_local = tok_dev // SEQ
    width = resid.shape[1]
    place_z = chip // (ny * nx)
    place_y = (chip // nx) % ny
    place_x = chip % nx

    def back(kz, ky, kx):
        row = ((place_z + nz - kz) % nz) * ny + (place_y + ny - ky) % ny
        return row * nx + (place_x + nx - kx) % nx

    slots_local = cache_state.shape[0]
    state_view = cache_state.reshape(slots_local, devices, per_dev, state_size)
    by_heads = lax.all_to_all(state_view, "wide", split_axis=1, concat_axis=0, tiled=True)
    by_heads = by_heads.reshape(-1, per_dev, state_size)

    weight_f = route_weight.astype(F32)
    share = weight_f / jnp.sum(weight_f, axis=-1, keepdims=True)
    expert_count = expert_home.shape[0]
    own_experts = expert_count // devices
    lookup = expert_ids[..., None] == jnp.arange(expert_count, dtype=jnp.int32)
    target = jnp.sum(jnp.where(lookup, expert_home, 0), axis=-1)
    by_row = jnp.sum(
        jnp.where(
            target[..., None] == jnp.arange(expert_count, dtype=jnp.int32), share[..., None], 0.0
        ),
        axis=1,
    )
    coarse = by_row.astype(BF16)
    fine = (by_row - coarse.astype(F32)).astype(BF16)
    known = jnp.concatenate([ssd_c, dt_raw, coarse, fine], axis=1)
    known = jnp.pad(known, ((0, 0), (0, -known.shape[1] % 128)))[None]
    known = moves.doubled(moves.doubled(moves.doubled(known, CORE), X), Y)
    known = moves.z_ring(known)
    near = jnp.arange(ny * nx * 2, dtype=jnp.int32)
    rel_order = jnp.concatenate(
        [
            back(kz, near // (2 * nx), (near // 2) % nx) * 2 + (core + near) % 2
            for kz in range(nz)
        ]
    )
    c_rel = jnp.concatenate([k[..., :state_size] for k in known], axis=0)
    c_rel = c_rel.reshape(devices, req_local, SEQ, state_size)
    shares = [
        jnp.concatenate(
            [known[kz][2 * (ky * nx + kx), :, state_size:] for ky, kx in moves.offsets(kz)], axis=0
        )
        for kz in range(nz)
    ]

    weights = []
    for swap in (False, True):
        for e in range(own_experts):
            weights += [moves.turn(w[e], CORE) if swap else w[e] for w in (w_gate, w_up, w_down)]
    near_lane = jnp.arange(own_experts, dtype=jnp.int32)
    lanes = jnp.concatenate(
        [me * own_experts + near_lane, (me + 1 - 2 * core) * own_experts + near_lane]
    )
    lanes = heads_all + lanes

    w_rows = moves.plane(w_out, 0)
    w_rows = w_rows + [moves.turn(a, CORE) for a in w_rows]
    order = jnp.stack(
        [
            (back(0, ky, kx) % (ny * nx)) * 2 + c
            for c in (core, 1 - core)
            for ky, kx in moves.offsets(0)
        ]
    )

    rates = -jnp.exp(a_log)
    local_step, local_cum = head_steps(dt_raw, dt_bias, rates, req_local)
    intra = intra_terms(
        ssd_x.reshape(req_local, SEQ, heads_all, head_dim),
        local_step,
        local_cum,
        ssd_b.reshape(req_local, SEQ, state_size),
        ssd_c.reshape(req_local, SEQ, state_size),
        d_skip,
    )

    plane = ny * nx * 2
    plane_heads = heads_all // nz

    def by_plane(a):
        a = jnp.swapaxes(a.reshape(tok_dev, devices, per_dev), 0, 1)
        return a.reshape(nz, plane, tok_dev, per_dev)

    intra_z = jnp.stack([by_plane(intra.reshape(tok_dev, columns)), by_plane(ssd_z)], axis=1)
    terms = []
    for k in range(nz):
        term = lax.dynamic_index_in_dim(intra_z, (place_z + k) % nz, 0, keepdims=False)
        terms.append(moves.turn(term, Z, k) if k else term)
    dt_col = jnp.concatenate(
        [k[0][:, state_size : state_size + heads_all] for k in known], axis=0
    )
    at_head = place_z * plane_heads
    _, col_cum = head_steps(
        lax.dynamic_slice_in_dim(dt_col, at_head, plane_heads, axis=1),
        lax.dynamic_slice_in_dim(dt_bias, at_head, plane_heads),
        lax.dynamic_slice_in_dim(rates, at_head, plane_heads),
        nz * req_local,
    )
    grow = jnp.exp(col_cum).reshape(nz * tok_dev, plane_heads)
    grow = jnp.repeat(grow, head_dim, axis=1).reshape(nz * tok_dev, plane, per_dev)
    grow = jnp.swapaxes(grow, 0, 1)
    gain = lax.dynamic_slice_in_dim(
        norm_gain.reshape(devices, 1, per_dev), place_z * plane, plane, axis=0
    )

    by_heads, w_rows, weights, shares, grow = lax.optimization_barrier(
        (by_heads, w_rows, weights, shares, grow)
    )
    rel_place = (rel_order % plane) * nz + jnp.arange(devices, dtype=jnp.int32) // plane
    product = carried_terms(cache_owner, rel_order, rel_place, c_rel, by_heads)
    product = product.reshape(plane, nz * tok_dev, per_dev)
    groups = [[z * plane + i for i in range(plane)] for z in range(nz)]
    carried = lax.all_to_all(product, "wide", 0, 0, axis_index_groups=groups)
    gated, squares, sums = mixer(order, carried, grow, gain, terms, w_rows)

    square = squares[0]
    for k in range(1, nz):
        square = square + moves.turn(squares[k], Z, -k)
    scale = lax.rsqrt(jnp.sum(square, axis=-1, keepdims=True) / columns + 1e-05)
    wide_moe = resid.astype(F32) + scale * moves.z_fold(sums)
    normed = (
        wide_moe
        * lax.rsqrt(jnp.mean(wide_moe * wide_moe, axis=-1, keepdims=True) + 1e-05)
        * moe_gain
    ).astype(BF16)

    normed, gated = lax.optimization_barrier((normed, gated))
    home = jnp.stack([moves.turn(g, Z, -k) if k else g for k, g in enumerate(gated)])
    home = jnp.roll(home, place_z, axis=0).reshape(devices, tok_dev, per_dev)
    ssd_out = (jnp.swapaxes(home, 0, 1).astype(F32) * scale[..., None]).astype(BF16)
    ssd_out = ssd_out.reshape(tok_dev, columns)

    held = moves.z_ring(normed)
    parts = [None] * nz
    for group in [moves.z_steps[i : i + 2] for i in range(0, nz, 2)]:
        blocks = [moves.plane(held[kz], kz) for kz in group]
        share_rows = jnp.concatenate([shares[kz] for kz in group], axis=0)
        outs = experts(lanes, share_rows, weights, sum(blocks, []), expert_count)
        for kz, b in zip(group, blocks):
            parts[kz] = moves.plane_fold(outs[: len(b)], kz)
            outs = outs[len(b) :]
    moe_out = moves.z_fold(parts).astype(BF16)
    return (ssd_out, moe_out)


def solution(mesh):
    both = ("group", "wide")
    in_specs = (
        P(both, None),
        P(both, None),
        P(both, None),
        P(both, None),
        P(both, None),
        P(),
        P(),
        P(),
        P(),
        P(both, None, None, None),
        P("group"),
        P(both, None),
        P("wide", None),
        P(),
        P(both, None),
        P(both, None),
        P(),
        P("wide", None, None),
        P("wide", None, None),
        P("wide", None, None),
    )
    out_specs = (P(both, None), P(both, None))
    step = functools.partial(local, Moves(grid_of(mesh)))
    return jax.shard_map(step, mesh=mesh, in_specs=in_specs, out_specs=out_specs, check_vma=False)
```
